32 devices in a mesh: expert: 16 (over z, y, x), replica: 2 (over core).
Axes of the slice: x: 2, y: 2, z: 4, core: 2. Of those that a mesh axis runs over, the one named last changes fastest.
Arguments:
- tokens: bfloat16 [1024, 7168], P('expert', 'replica'), may hold values from -6 to 6
- routes: int32 [1024, 8], P('expert'), may hold values from 0 to 15, all different within a row; in each aligned block of 64 rows (0 to 63, 64 to 127, ...) at most 64 rows name the same one
- route_scores: float32 [1024, 8], P('expert'), may hold values from 0.05 to 1
- placement: int32 [16], replicated, may hold values from 0 to 15, each once
- w_in: bfloat16 [16, 7168, 2, 1024], P('expert', 'replica'), may hold values from -0.0625 to 0.0625
- w_out: bfloat16 [16, 1024, 7168], P('expert', None, 'replica'), may hold values from -0.1875 to 0.1875
Outputs:
- mixed: bfloat16 [1024, 7168], P('expert', 'replica')
The draws below stay inside these ranges and needn't reach their ends.
Inputs may be any that keep to these rules, and one draw needn't show every extreme that they name: `routes`: each row names 8 different logical experts. Among the 64 rows of each aligned block (the tokens of one index of the expert axis) no expert is named by more than 64 rows, a bound that some block reaches. `placement`: A permutation of the physical slots.
All inputs are finite; a program needn't handle non-finite values.
Results may differ from the reference program's by a relative error of at most 0.0057.
Values may be sent and summed in bfloat16 or wider, within the bound.
A program may use at most 128 MiB of HBM per device.

```python
import math
import jax
import jax.numpy as jnp
import numpy as np
from jax import lax

D = 7168
FF = 1024
TOP = 8
TOK_DEV = 64
EXPERTS = 16
CAP = 64
TOKENS = 1024
N_EXPERT = 16


def block_levels(own_key, extent, split, smallest, largest):
    gain = 1.0
    for axis_at, blocks in split:
        heights = jax.random.uniform(jax.random.fold_in(jax.random.fold_in(own_key, 6), axis_at), (blocks,), jnp.float32, smallest / len(split), largest / len(split))
        gain = gain * jnp.repeat(jnp.exp(heights), extent[axis_at] // blocks).reshape((-1,) + (1,) * (len(extent) - 1 - axis_at))
    return gain


def shared_out(rng, own, number, rows, count, top, reach, skew):
    sequence = jax.random.permutation(rng, count)
    crowded, ordinary = load_shares(count, rows * top, reach, skew, True), load_shares(count, rows * top, reach, skew, False)
    places = jnp.arange(count)

    def named(lengths, turn):
        used = int((lengths > 0).sum())
        fixed = max(1, used // 4)
        passed = fixed + (places - fixed + turn * (used - fixed)) % max(1, count - fixed)
        return jnp.zeros((count,), jnp.int32).at[sequence[jnp.where(places < fixed, places, passed)]].set(jnp.asarray(lengths, jnp.int32))

    lengths = jnp.where(number % 4 == 0, named(crowded, number // 4), named(ordinary, number - number // 4 - 1))
    mixed = jax.random.permutation(jax.random.fold_in(own, 3), count)
    source_of, taker = mixed[0:count // 2 * 2:2], mixed[1:count // 2 * 2:2]
    room = jnp.minimum(lengths[source_of] - 1, reach - lengths[taker]) // 2
    room = jnp.where((source_of == sequence[0]) | (taker == sequence[0]) | (lengths[taker] == 0), 0, jnp.maximum(room, 0))
    passed = jax.random.randint(jax.random.fold_in(own, 4), (count // 2,), 0, 1 << 20) % (room + 1)
    lengths = lengths.at[source_of].add(-passed).at[taker].add(passed)
    items = jnp.searchsorted(jnp.cumsum(lengths), jnp.arange(rows * top), side="right").astype(jnp.int32)
    listing = items.reshape(top, rows).T
    listing = listing[jax.random.permutation(jax.random.fold_in(own, 1), rows)]
    turn = jax.random.randint(jax.random.fold_in(own, 2), (rows, 1), 0, top)
    return jnp.take_along_axis(listing, (jnp.arange(top)[None, :] + turn) % top, axis=1)


def load_shares(number_of, total, reach, slope, full):
    weights = [(1 << 20) // math.isqrt(standing ** slope) + 1 for standing in range(1, number_of + 1)]
    largest = reach if full else min(reach, max(-(-total // number_of), total * weights[0] // sum(weights)))
    least = 1 if total - largest >= number_of - 1 else 0
    counts, rest = [largest] + [least] * (number_of - 1), total - largest - least * (number_of - 1)
    while rest > 0:
        free = [i for i in range(1, number_of) if counts[i] < largest] or [i for i in range(1, number_of) if counts[i] < reach]
        pool, budget = sum([weights[i] for i in free]), rest
        for i in free:
            addition = min(reach - counts[i], max(1, budget * weights[i] // pool), rest)
            counts[i] = counts[i] + addition
            rest = rest - addition
    return np.array(counts)


def centred(own_key, dims, spread, reach, cuts=(), held_as=jnp.bfloat16):
    values = spread * jax.random.normal(own_key, dims, jnp.float32)
    if cuts:
        values = values * block_levels(own_key, dims, cuts, -0.22, 0.18)
    return jnp.clip(values, -reach, reach).astype(held_as)


def setup_inputs(seed: int = 0) -> dict:
    splits = jax.random.split(jax.random.key(seed), 7)
    tokens = centred(splits[0], (TOKENS, D), 1.0, 6.0, ((0, 16), (1, 2)))
    routes_keys = jax.random.split(jax.random.fold_in(splits[1], 1), TOKENS // TOK_DEV)
    routes_turns = jax.random.permutation(jax.random.fold_in(splits[1], 3), TOKENS // TOK_DEV)
    routes = jax.vmap(lambda own, number: shared_out(jax.random.fold_in(splits[1], 2), own, number, TOK_DEV, EXPERTS, TOP, CAP, 2))(routes_keys, routes_turns).reshape((TOKENS, TOP))
    route_scores = jnp.clip(jnp.exp(math.log(1.0) - 2.9957323 * jax.random.uniform(splits[2], (TOKENS, TOP), jnp.float32) ** block_levels(splits[2], (TOKENS, TOP), ((0, 16),), -0.2, 0.2)), 0.05, 1.0)
    placement = jax.random.permutation(splits[3], EXPERTS).astype(jnp.int32)
    w_in = centred(splits[4], (EXPERTS, D, 2, FF), D ** -0.5, 0.0625, ((0, 16), (1, 2)))
    w_out = centred(splits[5], (EXPERTS, FF, D), FF ** -0.5, 0.1875, ((0, 16), (2, 2)))
    return dict(tokens=tokens, routes=routes, route_scores=route_scores, placement=placement, w_in=w_in, w_out=w_out)


def reference(tokens, routes, route_scores, placement, w_in, w_out):
    physical = placement[routes]
    route_weight = 2.5 * route_scores / jnp.sum(route_scores, axis=1, keepdims=True)
    bound = N_EXPERT * CAP
    feature_cols = tokens.shape[1]

    def accumulate(running, expert):
        chosen = physical == expert
        member_weight = jnp.sum(jnp.where(chosen, route_weight, jnp.float32(0.0)), axis=1)
        taken = jnp.any(chosen, axis=1)
        members = jnp.nonzero(taken, size=bound, fill_value=0)[0]
        filled = jnp.arange(bound) < jnp.sum(taken.astype(jnp.int32))
        gathered = tokens[members]
        weights_in = lax.dynamic_index_in_dim(w_in, expert, 0, keepdims=False).reshape(feature_cols, 2 * FF)
        weights_out = lax.dynamic_index_in_dim(w_out, expert, 0, keepdims=False)
        pre_act = jnp.dot(gathered, weights_in, preferred_element_type=jnp.float32).reshape(bound, 2, FF)
        active = (jax.nn.silu(pre_act[:, 0]) * pre_act[:, 1]).astype(jnp.bfloat16)
        expert_out = jnp.dot(active, weights_out, preferred_element_type=jnp.float32).astype(jnp.bfloat16)
        expert_out = lax.optimization_barrier(expert_out).astype(jnp.float32)
        scale = jnp.where(filled, member_weight[members], jnp.float32(0.0))
        return running.at[members].add(expert_out * scale[:, None]), None

    mixed, unused = lax.scan(accumulate, jnp.zeros(tokens.shape, jnp.float32), jnp.arange(EXPERTS, dtype=jnp.int32))
    return mixed.astype(jnp.bfloat16)
```

```python
import jax
import jax.numpy as jnp
from jax import lax
from jax.sharding import PartitionSpec as P


def packed(tokens, routes, route_scores, placement, w_in, w_out):
    tok_rows, feature_cols = tokens.shape
    route_count = routes.shape[1]
    experts = placement.shape[0]
    hidden_units = w_in.shape[3]
    capacity = min(tok_rows, max(2, 2 * tok_rows * route_count // experts))
    slot_total = experts * capacity
    expert_ids = jnp.arange(experts, dtype=jnp.int32)
    route_table = routes[:, :, None] == expert_ids
    physical = jnp.sum(jnp.where(route_table, placement, 0), axis=-1)
    flat_slots = physical.reshape(-1)
    onehot = (flat_slots[:, None] == expert_ids).astype(jnp.int32)
    earlier = jnp.sum((jnp.cumsum(onehot, axis=0) - onehot) * onehot, axis=1)
    position = (flat_slots * capacity + earlier).reshape(tok_rows, route_count)
    slot_index = jnp.arange(slot_total, dtype=jnp.int32)
    placing = jnp.any(position[None, :, :] == slot_index[:, None, None], axis=-1).astype(
        jnp.bfloat16
    )
    outgoing = jnp.dot(placing, tokens, preferred_element_type=jnp.float32).astype(jnp.bfloat16)
    incoming = lax.all_to_all(outgoing, "expert", split_axis=0, concat_axis=0, tiled=True)
    weights_in = w_in[0].reshape(feature_cols, 2 * hidden_units)
    weights_out = w_out[0]
    partial_value = jnp.dot(incoming, weights_in, preferred_element_type=jnp.float32)
    partial_value = partial_value.reshape(slot_total, 2, hidden_units)
    shares = lax.psum_scatter(partial_value, "replica", scatter_dimension=2, tiled=True)
    active = (jax.nn.silu(shares[:, 0]) * shares[:, 1]).astype(jnp.bfloat16)
    result = jnp.dot(
        lax.all_gather(active, "replica", axis=1, tiled=True),
        weights_out,
        preferred_element_type=jnp.float32,
    )
    expert_out = result.astype(jnp.bfloat16)
    returned = lax.all_to_all(expert_out, "expert", split_axis=0, concat_axis=0, tiled=True)
    route_weight = 2.5 * route_scores / jnp.sum(route_scores, axis=1, keepdims=True)
    picked = returned[position.reshape(-1)].reshape(tok_rows, route_count, feature_cols)
    mixed = jnp.sum(picked.astype(jnp.float32) * route_weight[:, :, None], axis=1)
    return mixed.astype(jnp.bfloat16)


def expert_weights(routes, route_scores, placement):
    experts = placement.shape[0]
    expert_ids = jnp.arange(experts, dtype=jnp.int32)
    physical = jnp.sum(jnp.where(routes[:, :, None] == expert_ids, placement, 0), axis=-1)
    route_weight = 2.5 * route_scores / jnp.sum(route_scores, axis=1, keepdims=True)
    return jnp.sum(
        jnp.where(physical[:, :, None] == expert_ids, route_weight[:, :, None], 0.0), axis=1
    )


def dense(tokens, routes, route_scores, placement, w_in, w_out):
    feature_cols = tokens.shape[1]
    hidden_units = w_in.shape[3]
    table = expert_weights(routes, route_scores, placement)
    mine = lax.all_to_all(table, "expert", split_axis=1, concat_axis=0, tiled=True)
    incoming = lax.all_gather(tokens, "expert", axis=0, tiled=True)
    rows = incoming.shape[0]
    weights_in = w_in[0].reshape(feature_cols, 2 * hidden_units)
    partial_value = jnp.dot(incoming, weights_in, preferred_element_type=jnp.float32)
    partial_value = partial_value.reshape(rows, 2, hidden_units)
    shares = lax.psum_scatter(partial_value, "replica", scatter_dimension=2, tiled=True)
    active = (jax.nn.silu(shares[:, 0]) * shares[:, 1]).astype(jnp.bfloat16)
    result = jnp.dot(
        lax.all_gather(active, "replica", axis=1, tiled=True),
        w_out[0],
        preferred_element_type=jnp.float32,
    )
    weighted = (result.astype(jnp.bfloat16).astype(jnp.float32) * mine).astype(jnp.bfloat16)
    return lax.psum_scatter(weighted, "expert", scatter_dimension=0, tiled=True)


def on_device(tokens, routes, route_scores, placement, w_in, w_out):
    tok_rows = tokens.shape[0]
    if 2 * tok_rows * routes.shape[1] // placement.shape[0] >= tok_rows:
        return dense(tokens, routes, route_scores, placement, w_in, w_out)
    return packed(tokens, routes, route_scores, placement, w_in, w_out)


def solution(mesh):
    in_specs = (
        P("expert", "replica"),
        P("expert", None),
        P("expert", None),
        P(),
        P("expert", "replica", None, None),
        P("expert", None, "replica"),
    )
    out_specs = P("expert", "replica")
    return jax.shard_map(
        on_device, mesh=mesh, in_specs=in_specs, out_specs=out_specs, check_vma=False
    )
```

```python
import jax
import jax.numpy as jnp
from jax import lax
from jax.experimental import pallas as pl
from jax.experimental.pallas import tpu as pltpu
from jax.sharding import PartitionSpec as P

LANES = 128
TILE = 256
MESH = pl.DeviceIdType.MESH
LINE = 4


def packed(tokens, routes, route_scores, placement, w_in, w_out):
    tok_rows, feature_cols = tokens.shape
    route_count = routes.shape[1]
    experts = placement.shape[0]
    hidden_units = w_in.shape[3]
    capacity = min(tok_rows, max(2, 2 * tok_rows * route_count // experts))
    slot_total = experts * capacity
    expert_ids = jnp.arange(experts, dtype=jnp.int32)
    route_table = routes[:, :, None] == expert_ids
    physical = jnp.sum(jnp.where(route_table, placement, 0), axis=-1)
    flat_slots = physical.reshape(-1)
    onehot = (flat_slots[:, None] == expert_ids).astype(jnp.int32)
    earlier = jnp.sum((jnp.cumsum(onehot, axis=0) - onehot) * onehot, axis=1)
    position = (flat_slots * capacity + earlier).reshape(tok_rows, route_count)
    slot_index = jnp.arange(slot_total, dtype=jnp.int32)
    placing = jnp.any(position[None, :, :] == slot_index[:, None, None], axis=-1).astype(
        jnp.bfloat16
    )
    outgoing = jnp.dot(placing, tokens, preferred_element_type=jnp.float32).astype(jnp.bfloat16)
    incoming = lax.all_to_all(outgoing, "expert", split_axis=0, concat_axis=0, tiled=True)
    weights_in = w_in[0].reshape(feature_cols, 2 * hidden_units)
    weights_out = w_out[0]
    partial_value = jnp.dot(incoming, weights_in, preferred_element_type=jnp.float32)
    partial_value = partial_value.reshape(slot_total, 2, hidden_units)
    shares = lax.psum_scatter(partial_value, "replica", scatter_dimension=2, tiled=True)
    active = (jax.nn.silu(shares[:, 0]) * shares[:, 1]).astype(jnp.bfloat16)
    result = jnp.dot(
        lax.all_gather(active, "replica", axis=1, tiled=True),
        weights_out,
        preferred_element_type=jnp.float32,
    )
    expert_out = result.astype(jnp.bfloat16)
    returned = lax.all_to_all(expert_out, "expert", split_axis=0, concat_axis=0, tiled=True)
    route_weight = 2.5 * route_scores / jnp.sum(route_scores, axis=1, keepdims=True)
    picked = returned[position.reshape(-1)].reshape(tok_rows, route_count, feature_cols)
    mixed = jnp.sum(picked.astype(jnp.float32) * route_weight[:, :, None], axis=1)
    return mixed.astype(jnp.bfloat16)


def expert_weights(routes, route_scores, placement):
    experts = placement.shape[0]
    expert_ids = jnp.arange(experts, dtype=jnp.int32)
    physical = jnp.sum(jnp.where(routes[:, :, None] == expert_ids, placement, 0), axis=-1)
    route_weight = 2.5 * route_scores / jnp.sum(route_scores, axis=1, keepdims=True)
    return jnp.sum(
        jnp.where(physical[:, :, None] == expert_ids, route_weight[:, :, None], 0.0), axis=1
    )


def layer_kernel(
    ext_ref, w_in_ref, w_out_ref, out_ref,
    xs, wg, wu, stage, wo, contrib, from_b, from_a, from_z, part, sent, got, act,
    w_sem, wo_sem, z_send, a_send, b_send, x_recv,
    p_send, p_recv, rb_send, rb_recv, ra_send, ra_recv, rz_send, rz_recv,
):
    rows, width = ext_ref.shape
    cols = out_ref.shape[1]
    hidden = wg.shape[1]
    tiles = hidden // TILE
    me = lax.axis_index("expert")
    core = lax.axis_index("replica")
    x, y, z = me % 2, (me // 2) % 2, me // 4
    flip_x, flip_y = me + 1 - 2 * x, me + 2 - 4 * y
    near_a = (1 - core) * flip_x + core * flip_y
    near_b = (1 - core) * flip_y + core * flip_x
    base = me - 4 * z

    def line(d):
        return (z + d) % LINE

    barrier = pltpu.get_barrier_semaphore()
    peers = [(near_a, core), (near_b, core), (me, 1 - core)]
    peers += [(base + 4 * line(d), core) for d in range(1, LINE)]
    for peer in peers:
        pl.semaphore_signal(barrier, inc=1, device_id=peer, device_id_type=MESH)
    pl.semaphore_wait(barrier, len(peers))

    def remote(src, dst, send, recv, chip, on_core=None):
        return pltpu.make_async_remote_copy(
            src_ref=src, dst_ref=dst, send_sem=send, recv_sem=recv,
            device_id=(chip, core if on_core is None else on_core), device_id_type=MESH,
        )

    def arrived(ref, recv):
        remote(ref, ref, a_send.at[0], recv, near_a).wait_recv()

    def stage_copy(ct):
        return pltpu.make_async_copy(
            w_in_ref.at[0, :, :, pl.ds(ct * LANES, LANES)], stage.at[ct % 2], w_sem.at[ct % 2]
        )

    pending = []

    def go(copy):
        copy.start()
        pending.append(copy)

    go(remote(ext_ref, xs.at[LINE + z], a_send.at[0], x_recv.at[LINE + z], near_a))
    go(remote(ext_ref, xs.at[2 * LINE + z], b_send.at[0], x_recv.at[2 * LINE + z], near_b))
    for d in (1, 3, 2):
        go(remote(ext_ref, xs.at[z], z_send.at[d - 1], x_recv.at[z], base + 4 * line(d)))
    stage_copy(0).start()
    stage_copy(1).start()
    out_weights = pltpu.make_async_copy(w_out_ref.at[0], wo, wo_sem)
    out_weights.start()
    xs[z] = ext_ref[...]

    row = lax.broadcasted_iota(jnp.int32, (TILE, TILE), 0)
    col = lax.broadcasted_iota(jnp.int32, (TILE, TILE), 1)
    half = TILE // 2
    wanted = jnp.where(row < half, 2 * row, 2 * (row - half) + 1)
    sorter = (col == wanted).astype(jnp.float32).astype(jnp.bfloat16)

    def sort_tile(ct):
        stage_copy(ct).wait()
        flat = stage.at[ct % 2].reshape(2 * cols, LANES)

        def body(k, carry):
            piece = flat[pl.ds(pl.multiple_of(k * TILE, TILE), TILE), :]
            both = jnp.dot(sorter, piece, preferred_element_type=jnp.float32).astype(jnp.bfloat16)
            at = pl.ds(pl.multiple_of(k * half, half), half)
            wg[at, ct * LANES:(ct + 1) * LANES] = both[:half]
            wu[at, ct * LANES:(ct + 1) * LANES] = both[half:]
            return carry

        lax.fori_loop(0, 2 * cols // TILE, body, 0)
        if ct + 2 < hidden // LANES:
            stage_copy(ct + 2).start()

    def own_line_on(d, n):
        slot = line(d)
        arrived(xs.at[slot], x_recv.at[slot])
        go(remote(xs.at[slot], xs.at[LINE + slot], a_send.at[n], x_recv.at[LINE + slot], near_a))
        to = 2 * LINE + slot
        go(remote(xs.at[slot], xs.at[to], b_send.at[n], x_recv.at[to], near_b))

    def a_line_on(d, n):
        slot = LINE + line(d)
        arrived(xs.at[slot], x_recv.at[slot])
        to = 2 * LINE + slot
        go(remote(xs.at[slot], xs.at[to], b_send.at[LINE + n], x_recv.at[to], near_b))

    all_tiles = list(range(hidden // LANES))
    quarter = max(1, len(all_tiles) // 4)
    for ct in all_tiles[:2 * quarter]:
        sort_tile(ct)
    own_line_on(1, 1)
    a_line_on(0, 0)
    for ct in all_tiles[2 * quarter:3 * quarter]:
        sort_tile(ct)
    own_line_on(3, 2)
    a_line_on(1, 1)
    for ct in all_tiles[3 * quarter:]:
        sort_tile(ct)
    own_line_on(2, 3)
    a_line_on(3, 2)
    a_line_on(2, 3)
    out_weights.wait()

    lane = lax.broadcasted_iota(jnp.int32, (LINE * rows, LANES), 1)
    mine = (lane % 16 == me) & (lane < 48)

    def exchange(s, j):
        return remote(sent.at[s, j], got.at[s, j], p_send.at[s, j], p_recv.at[s, j], me, 1 - core)

    def step(s, group):
        block = pl.ds(group * LINE, LINE)

        def first(j, carry):
            at = pl.ds(pl.multiple_of(j * TILE, TILE), TILE)
            value = xs[block, :, :cols].reshape(LINE * rows, cols)
            gate = jnp.dot(value, wg[:, at], preferred_element_type=jnp.float32)
            up = jnp.dot(value, wu[:, at], preferred_element_type=jnp.float32)
            part[j, 0] = gate
            part[j, 1] = up
            sent[s, j, 0] = gate.astype(jnp.bfloat16)
            sent[s, j, 1] = up.astype(jnp.bfloat16)
            exchange(s, j).start()
            return carry

        lax.fori_loop(0, tiles, first, 0)

        def second(j, carry):
            exchange(s, j).wait_recv()
            gate = part[j, 0] + got[s, j, 0].astype(jnp.float32)
            up = part[j, 1] + got[s, j, 1].astype(jnp.float32)
            act[:, pl.ds(pl.multiple_of(j * TILE, TILE), TILE)] = (
                gate / (1.0 + jnp.exp(-gate)) * up
            ).astype(jnp.bfloat16)
            return carry

        lax.fori_loop(0, tiles, second, 0)
        scales = xs[block, :, cols:].reshape(LINE * rows, LANES).astype(jnp.float32)
        scale = jnp.sum(jnp.where(mine, scales, 0.0), axis=1, keepdims=True)

        def third(j, carry):
            at = pl.ds(pl.multiple_of(j * TILE, TILE), TILE)
            value = jnp.dot(act[...], wo[:, at], preferred_element_type=jnp.float32)
            value = value.astype(jnp.bfloat16).astype(jnp.float32) * scale
            contrib[block, :, at] = value.astype(jnp.bfloat16).reshape(LINE, rows, TILE)
            return carry

        lax.fori_loop(0, cols // TILE, third, 0)

    step(0, 0)
    for d in range(LINE):
        slot = 2 * LINE + line(d)
        arrived(xs.at[slot], x_recv.at[slot])
    step(1, 1 + core)
    step(2, 2 - core)
    order = (1, 3, 2, 0)
    for n, d in enumerate(order):
        src = 2 * LINE + line(d)
        to = line(d)
        go(remote(contrib.at[src], from_b.at[to], rb_send.at[n], rb_recv.at[to], near_b))
    for d in range(LINE):
        slot = 3 * LINE + line(d)
        arrived(xs.at[slot], x_recv.at[slot])
    step(3, 3)
    for n, d in enumerate(order):
        src = 3 * LINE + line(d)
        to = LINE + line(d)
        go(remote(contrib.at[src], from_b.at[to], rb_send.at[LINE + n], rb_recv.at[to], near_b))

    def plus(values):
        total = values[0].astype(jnp.float32)
        for value in values[1:]:
            total = total + value.astype(jnp.float32)
        return total

    for n, d in enumerate(order):
        slot = LINE + line(d)
        arrived(from_b.at[slot], rb_recv.at[slot])
        contrib[slot] = plus([contrib[slot], from_b[slot]]).astype(jnp.bfloat16)
        to = line(d)
        go(remote(contrib.at[slot], from_a.at[to], ra_send.at[n], ra_recv.at[to], near_a))
    for n, d in enumerate(order):
        slot = line(d)
        arrived(from_b.at[slot], rb_recv.at[slot])
        arrived(from_a.at[slot], ra_recv.at[slot])
        total = plus([contrib[slot], from_b[slot], from_a[slot]])
        if d:
            contrib[slot] = total.astype(jnp.bfloat16)
            to = LINE - 1 - d
            chip = base + 4 * slot
            go(remote(contrib.at[slot], from_z.at[to], rz_send.at[n], rz_recv.at[to], chip))
        else:
            contrib[slot] = total.astype(jnp.bfloat16)
    for d in range(LINE - 1):
        arrived(from_z.at[d], rz_recv.at[d])
    out_ref[...] = plus([contrib[z], from_z[0], from_z[1], from_z[2]]).astype(jnp.bfloat16)
    for copy in pending:
        copy.wait_send()

    def drain(n, carry):
        exchange(n // tiles, n % tiles).wait_send()
        return carry

    lax.fori_loop(0, LINE * tiles, drain, 0)


def fused(tokens, routes, route_scores, placement, w_in, w_out):
    rows, cols = tokens.shape
    hidden = w_in.shape[3]
    tiles = hidden // TILE
    table = expert_weights(routes, route_scores, placement)
    high = lax.reduce_precision(table, 8, 7)
    middle = lax.reduce_precision(table - high, 8, 7)
    low = table - high - middle
    thirds = [third.astype(jnp.bfloat16) for third in (high, middle, low)]
    filler = jnp.zeros((rows, LANES - 3 * table.shape[1]), jnp.bfloat16)
    ext = jnp.concatenate([tokens, *thirds, filler], axis=1)
    slots = LINE * LINE
    bf16 = jnp.bfloat16
    dma = pltpu.SemaphoreType.DMA
    return pl.pallas_call(
        layer_kernel,
        out_shape=jax.ShapeDtypeStruct((rows, cols), bf16),
        in_specs=[
            pl.BlockSpec(memory_space=pltpu.VMEM),
            pl.BlockSpec(memory_space=pl.ANY),
            pl.BlockSpec(memory_space=pl.ANY),
        ],
        out_specs=pl.BlockSpec(memory_space=pltpu.VMEM),
        scratch_shapes=[
            pltpu.VMEM((slots, rows, cols + LANES), bf16),
            pltpu.VMEM((cols, hidden), bf16),
            pltpu.VMEM((cols, hidden), bf16),
            pltpu.VMEM((2, cols, 2, LANES), bf16),
            pltpu.VMEM((hidden, cols), bf16),
            pltpu.VMEM((slots, rows, cols), bf16),
            pltpu.VMEM((2 * LINE, rows, cols), bf16),
            pltpu.VMEM((LINE, rows, cols), bf16),
            pltpu.VMEM((LINE - 1, rows, cols), bf16),
            pltpu.VMEM((tiles, 2, LINE * rows, TILE), jnp.float32),
            pltpu.VMEM((LINE, tiles, 2, LINE * rows, TILE), bf16),
            pltpu.VMEM((LINE, tiles, 2, LINE * rows, TILE), bf16),
            pltpu.VMEM((LINE * rows, hidden), bf16),
            dma((2,)), dma, dma((LINE - 1,)), dma((LINE,)), dma((2 * LINE,)), dma((slots,)),
            dma((LINE, tiles)), dma((LINE, tiles)),
            dma((2 * LINE,)), dma((2 * LINE,)), dma((LINE,)), dma((LINE,)),
            dma((LINE,)), dma((LINE - 1,)),
        ],
        compiler_params=pltpu.CompilerParams(
            collective_id=0, has_side_effects=True, vmem_limit_bytes=67043328
        ),
    )(ext, w_in, w_out)


def on_device(tokens, routes, route_scores, placement, w_in, w_out):
    tok_rows = tokens.shape[0]
    experts = placement.shape[0]
    fits = experts == 4 * LINE and lax.axis_size("replica") == 2
    if fits and 2 * tok_rows * routes.shape[1] // experts >= tok_rows:
        return fused(tokens, routes, route_scores, placement, w_in, w_out)
    return packed(tokens, routes, route_scores, placement, w_in, w_out)


def solution(mesh):
    in_specs = (
        P("expert", "replica"),
        P("expert", None),
        P("expert", None),
        P(),
        P("expert", "replica", None, None),
        P("expert", None, "replica"),
    )
    out_specs = P("expert", "replica")
    return jax.shard_map(
        on_device, mesh=mesh, in_specs=in_specs, out_specs=out_specs, check_vma=False
    )
```

```python
import jax
import jax.numpy as jnp
from jax import lax
from jax.experimental import pallas as pl
from jax.experimental.pallas import tpu as pltpu
from jax.sharding import PartitionSpec as P

LANES = 128
TILE = 256
MESH = pl.DeviceIdType.MESH
LINE = 4


def packed(tokens, routes, route_scores, placement, w_in, w_out):
    tok_rows, feature_cols = tokens.shape
    route_count = routes.shape[1]
    experts = placement.shape[0]
    hidden_units = w_in.shape[3]
    capacity = min(tok_rows, max(2, 2 * tok_rows * route_count // experts))
    slot_total = experts * capacity
    expert_ids = jnp.arange(experts, dtype=jnp.int32)
    route_table = routes[:, :, None] == expert_ids
    physical = jnp.sum(jnp.where(route_table, placement, 0), axis=-1)
    flat_slots = physical.reshape(-1)
    onehot = (flat_slots[:, None] == expert_ids).astype(jnp.int32)
    earlier = jnp.sum((jnp.cumsum(onehot, axis=0) - onehot) * onehot, axis=1)
    position = (flat_slots * capacity + earlier).reshape(tok_rows, route_count)
    slot_index = jnp.arange(slot_total, dtype=jnp.int32)
    placing = jnp.any(position[None, :, :] == slot_index[:, None, None], axis=-1).astype(
        jnp.bfloat16
    )
    outgoing = jnp.dot(placing, tokens, preferred_element_type=jnp.float32).astype(jnp.bfloat16)
    incoming = lax.all_to_all(outgoing, "expert", split_axis=0, concat_axis=0, tiled=True)
    weights_in = w_in[0].reshape(feature_cols, 2 * hidden_units)
    weights_out = w_out[0]
    partial_value = jnp.dot(incoming, weights_in, preferred_element_type=jnp.float32)
    partial_value = partial_value.reshape(slot_total, 2, hidden_units)
    shares = lax.psum_scatter(partial_value, "replica", scatter_dimension=2, tiled=True)
    active = (jax.nn.silu(shares[:, 0]) * shares[:, 1]).astype(jnp.bfloat16)
    result = jnp.dot(
        lax.all_gather(active, "replica", axis=1, tiled=True),
        weights_out,
        preferred_element_type=jnp.float32,
    )
    expert_out = result.astype(jnp.bfloat16)
    returned = lax.all_to_all(expert_out, "expert", split_axis=0, concat_axis=0, tiled=True)
    route_weight = 2.5 * route_scores / jnp.sum(route_scores, axis=1, keepdims=True)
    picked = returned[position.reshape(-1)].reshape(tok_rows, route_count, feature_cols)
    mixed = jnp.sum(picked.astype(jnp.float32) * route_weight[:, :, None], axis=1)
    return mixed.astype(jnp.bfloat16)


def expert_weights(routes, route_scores, placement):
    experts = placement.shape[0]
    expert_ids = jnp.arange(experts, dtype=jnp.int32)
    physical = jnp.sum(jnp.where(routes[:, :, None] == expert_ids, placement, 0), axis=-1)
    route_weight = 2.5 * route_scores / jnp.sum(route_scores, axis=1, keepdims=True)
    return jnp.sum(
        jnp.where(physical[:, :, None] == expert_ids, route_weight[:, :, None], 0.0), axis=1
    )


def layer_kernel(
    ext_ref, w_in_ref, w_out_ref, out_ref,
    xs, wg, wu, stage, wo, contrib, from_b, from_a, from_z, part, sent, got, act,
    w_sem, wo_sem, z_send, a_send, b_send, x_recv,
    p_send, p_recv, rb_send, rb_recv, ra_send, ra_recv, rz_send, rz_recv,
):
    rows, width = ext_ref.shape
    cols = out_ref.shape[1]
    hidden = wg.shape[1]
    tiles = hidden // TILE
    me = lax.axis_index("expert")
    core = lax.axis_index("replica")
    x, y, z = me % 2, (me // 2) % 2, me // 4
    flip_x, flip_y = me + 1 - 2 * x, me + 2 - 4 * y
    near_a = (1 - core) * flip_x + core * flip_y
    near_b = (1 - core) * flip_y + core * flip_x
    base = me - 4 * z

    def line(d):
        return (z + d) % LINE

    barrier = pltpu.get_barrier_semaphore()
    peers = [(near_a, core), (near_b, core), (me, 1 - core)]
    peers += [(base + 4 * line(d), core) for d in range(1, LINE)]
    for peer in peers:
        pl.semaphore_signal(barrier, inc=1, device_id=peer, device_id_type=MESH)
    pl.semaphore_wait(barrier, len(peers))

    def remote(src, dst, send, recv, chip, on_core=None):
        return pltpu.make_async_remote_copy(
            src_ref=src, dst_ref=dst, send_sem=send, recv_sem=recv,
            device_id=(chip, core if on_core is None else on_core), device_id_type=MESH,
        )

    def arrived(ref, recv):
        remote(ref, ref, a_send.at[0, 0], recv, near_a).wait_recv()

    def stage_copy(ct):
        return pltpu.make_async_copy(
            w_in_ref.at[0, :, :, pl.ds(ct * LANES, LANES)], stage.at[ct % 2], w_sem.at[ct % 2]
        )

    pending = []

    def go(copy):
        copy.start()
        pending.append(copy)

    part_rows = rows // 2

    def pass_on(source, to, send, chip, h):
        part = pl.ds(h * part_rows, part_rows)
        go(remote(source, xs.at[to, part], send.at[h], x_recv.at[to, h], chip))

    def landed(slot, h):
        part = pl.ds(h * part_rows, part_rows)
        arrived(xs.at[slot, part], x_recv.at[slot, h])
        return xs.at[slot, part]

    for h in range(2):
        own = ext_ref.at[pl.ds(h * part_rows, part_rows)]
        pass_on(own, LINE + z, a_send.at[0], near_a, h)
        pass_on(own, 2 * LINE + z, b_send.at[0], near_b, h)
        for d in (1, 3, 2):
            pass_on(own, z, z_send.at[d - 1], base + 4 * line(d), h)
    stage_copy(0).start()
    stage_copy(1).start()
    out_weights = pltpu.make_async_copy(w_out_ref.at[0], wo, wo_sem)
    out_weights.start()
    xs[z] = ext_ref[...]

    row = lax.broadcasted_iota(jnp.int32, (TILE, TILE), 0)
    col = lax.broadcasted_iota(jnp.int32, (TILE, TILE), 1)
    half = TILE // 2
    wanted = jnp.where(row < half, 2 * row, 2 * (row - half) + 1)
    sorter = (col == wanted).astype(jnp.float32).astype(jnp.bfloat16)

    def sort_tile(ct):
        stage_copy(ct).wait()
        flat = stage.at[ct % 2].reshape(2 * cols, LANES)

        def body(k, carry):
            piece = flat[pl.ds(pl.multiple_of(k * TILE, TILE), TILE), :]
            both = jnp.dot(sorter, piece, preferred_element_type=jnp.float32).astype(jnp.bfloat16)
            at = pl.ds(pl.multiple_of(k * half, half), half)
            wg[at, ct * LANES:(ct + 1) * LANES] = both[:half]
            wu[at, ct * LANES:(ct + 1) * LANES] = both[half:]
            return carry

        lax.fori_loop(0, 2 * cols // TILE, body, 0)
        if ct + 2 < hidden // LANES:
            stage_copy(ct + 2).start()

    def own_line_on(d, n):
        slot = line(d)
        for h in range(2):
            held = landed(slot, h)
            pass_on(held, LINE + slot, a_send.at[n], near_a, h)
            pass_on(held, 2 * LINE + slot, b_send.at[n], near_b, h)

    def a_line_on(d, n):
        slot = LINE + line(d)
        for h in range(2):
            held = landed(slot, h)
            pass_on(held, 2 * LINE + slot, b_send.at[LINE + n], near_b, h)

    all_tiles = list(range(hidden // LANES))
    quarter = max(1, len(all_tiles) // 4)
    for ct in all_tiles[:2 * quarter]:
        sort_tile(ct)
    own_line_on(1, 1)
    a_line_on(0, 0)
    for ct in all_tiles[2 * quarter:3 * quarter]:
        sort_tile(ct)
    own_line_on(3, 2)
    a_line_on(1, 1)
    for ct in all_tiles[3 * quarter:]:
        sort_tile(ct)
    own_line_on(2, 3)
    a_line_on(3, 2)
    a_line_on(2, 3)
    out_weights.wait()

    lane = lax.broadcasted_iota(jnp.int32, (LINE * rows, LANES), 1)
    mine = (lane % 16 == me) & (lane < 48)

    def exchange(s, j):
        return remote(sent.at[s, j], got.at[s, j], p_send.at[s, j], p_recv.at[s, j], me, 1 - core)

    def step(s, group, ship=None):
        block = pl.ds(group * LINE, LINE)

        def first(j, carry):
            at = pl.ds(pl.multiple_of(j * TILE, TILE), TILE)
            value = xs[block, :, :cols].reshape(LINE * rows, cols)
            gate = jnp.dot(value, wg[:, at], preferred_element_type=jnp.float32)
            up = jnp.dot(value, wu[:, at], preferred_element_type=jnp.float32)
            part[j, 0] = gate
            part[j, 1] = up
            sent[s, j, 0] = gate.astype(jnp.bfloat16)
            sent[s, j, 1] = up.astype(jnp.bfloat16)
            exchange(s, j).start()
            return carry

        lax.fori_loop(0, tiles, first, 0)

        def second(j, carry):
            exchange(s, j).wait_recv()
            gate = part[j, 0] + got[s, j, 0].astype(jnp.float32)
            up = part[j, 1] + got[s, j, 1].astype(jnp.float32)
            act[:, pl.ds(pl.multiple_of(j * TILE, TILE), TILE)] = (
                gate / (1.0 + jnp.exp(-gate)) * up
            ).astype(jnp.bfloat16)
            return carry

        lax.fori_loop(0, tiles, second, 0)
        scales = xs[block, :, cols:].reshape(LINE * rows, LANES).astype(jnp.float32)
        scale = jnp.sum(jnp.where(mine, scales, 0.0), axis=1, keepdims=True)

        def third(j, carry):
            at = pl.ds(pl.multiple_of(j * TILE, TILE), TILE)
            value = jnp.dot(act[...], wo[:, at], preferred_element_type=jnp.float32)
            value = value * scale
            contrib[block, :, at] = value.astype(jnp.bfloat16).reshape(LINE, rows, TILE)
            return carry

        out_tiles = wide // TILE
        for h in range(2):
            lax.fori_loop(h * out_tiles, (h + 1) * out_tiles, third, 0)
            if ship is not None:
                ship(h)

    wide = cols // 2
    order = (1, 3, 2, 0)

    def cut(h):
        return slice(h * wide, (h + 1) * wide)

    def ship_b(from_line, to_line, h):
        for n, d in enumerate(order):
            src, to = from_line * LINE + line(d), to_line * LINE + line(d)
            go(remote(contrib.at[src, :, cut(h)], from_b.at[to, :, cut(h)],
                      rb_send.at[to_line * LINE + n, h], rb_recv.at[to, h], near_b))

    step(0, 0)
    for d in range(LINE):
        for h in range(2):
            landed(2 * LINE + line(d), h)
    step(1, 1 + core)
    step(2, 2 - core)
    for h in range(2):
        ship_b(2, 0, h)
    for d in range(LINE):
        for h in range(2):
            landed(3 * LINE + line(d), h)
    step(3, 3, lambda h: ship_b(3, 1, h))

    def plus(values):
        total = values[0].astype(jnp.float32)
        for value in values[1:]:
            total = total + value.astype(jnp.float32)
        return total

    def to_a(h, n, d):
        slot, to = LINE + line(d), line(d)
        arrived(from_b.at[slot, :, cut(h)], rb_recv.at[slot, h])
        contrib[slot, :, cut(h)] = plus(
            [contrib[slot, :, cut(h)], from_b[slot, :, cut(h)]]
        ).astype(jnp.bfloat16)
        go(remote(contrib.at[slot, :, cut(h)], from_a.at[to, :, cut(h)],
                  ra_send.at[n, h], ra_recv.at[to, h], near_a))

    def to_z(h, n, d):
        slot = line(d)
        arrived(from_b.at[slot, :, cut(h)], rb_recv.at[slot, h])
        arrived(from_a.at[slot, :, cut(h)], ra_recv.at[slot, h])
        contrib[slot, :, cut(h)] = plus(
            [contrib[slot, :, cut(h)], from_b[slot, :, cut(h)], from_a[slot, :, cut(h)]]
        ).astype(jnp.bfloat16)
        if d:
            to = LINE - 1 - d
            go(remote(contrib.at[slot, :, cut(h)], from_z.at[to, :, cut(h)],
                      rz_send.at[n, h], rz_recv.at[to, h], base + 4 * slot))

    for n, d in enumerate(order):
        to_a(0, n, d)
    for n, d in enumerate(order):
        to_a(1, n, d)
        to_z(0, n, d)
    for n, d in enumerate(order):
        to_z(1, n, d)
    for h in range(2):
        for d in range(LINE - 1):
            arrived(from_z.at[d, :, cut(h)], rz_recv.at[d, h])
        out_ref[:, cut(h)] = plus(
            [contrib[z, :, cut(h)]] + [from_z[d, :, cut(h)] for d in range(LINE - 1)]
        ).astype(jnp.bfloat16)
    for copy in pending:
        copy.wait_send()

    def drain(n, carry):
        exchange(n // tiles, n % tiles).wait_send()
        return carry

    lax.fori_loop(0, LINE * tiles, drain, 0)


def fused(tokens, routes, route_scores, placement, w_in, w_out):
    rows, cols = tokens.shape
    hidden = w_in.shape[3]
    tiles = hidden // TILE
    table = expert_weights(routes, route_scores, placement)
    high = lax.reduce_precision(table, 8, 7)
    middle = lax.reduce_precision(table - high, 8, 7)
    low = table - high - middle
    thirds = [third.astype(jnp.bfloat16) for third in (high, middle, low)]
    filler = jnp.zeros((rows, LANES - 3 * table.shape[1]), jnp.bfloat16)
    ext = jnp.concatenate([tokens, *thirds, filler], axis=1)
    slots = LINE * LINE
    bf16 = jnp.bfloat16
    dma = pltpu.SemaphoreType.DMA
    return pl.pallas_call(
        layer_kernel,
        out_shape=jax.ShapeDtypeStruct((rows, cols), bf16),
        in_specs=[
            pl.BlockSpec(memory_space=pltpu.VMEM),
            pl.BlockSpec(memory_space=pl.ANY),
            pl.BlockSpec(memory_space=pl.ANY),
        ],
        out_specs=pl.BlockSpec(memory_space=pltpu.VMEM),
        scratch_shapes=[
            pltpu.VMEM((slots, rows, cols + LANES), bf16),
            pltpu.VMEM((cols, hidden), bf16),
            pltpu.VMEM((cols, hidden), bf16),
            pltpu.VMEM((2, cols, 2, LANES), bf16),
            pltpu.VMEM((hidden, cols), bf16),
            pltpu.VMEM((slots, rows, cols), bf16),
            pltpu.VMEM((2 * LINE, rows, cols), bf16),
            pltpu.VMEM((LINE, rows, cols), bf16),
            pltpu.VMEM((LINE - 1, rows, cols), bf16),
            pltpu.VMEM((tiles, 2, LINE * rows, TILE), jnp.float32),
            pltpu.VMEM((LINE, tiles, 2, LINE * rows, TILE), bf16),
            pltpu.VMEM((LINE, tiles, 2, LINE * rows, TILE), bf16),
            pltpu.VMEM((LINE * rows, hidden), bf16),
            dma((2,)), dma, dma((LINE - 1, 2)), dma((LINE, 2)), dma((2 * LINE, 2)), dma((slots, 2)),
            dma((LINE, tiles)), dma((LINE, tiles)),
            dma((2 * LINE, 2)), dma((2 * LINE, 2)), dma((LINE, 2)), dma((LINE, 2)),
            dma((LINE, 2)), dma((LINE - 1, 2)),
        ],
        compiler_params=pltpu.CompilerParams(
            collective_id=0, has_side_effects=True, vmem_limit_bytes=67043328
        ),
    )(ext, w_in, w_out)


def on_device(tokens, routes, route_scores, placement, w_in, w_out):
    tok_rows = tokens.shape[0]
    experts = placement.shape[0]
    fits = experts == 4 * LINE and lax.axis_size("replica") == 2
    if fits and 2 * tok_rows * routes.shape[1] // experts >= tok_rows:
        return fused(tokens, routes, route_scores, placement, w_in, w_out)
    return packed(tokens, routes, route_scores, placement, w_in, w_out)


def solution(mesh):
    in_specs = (
        P("expert", "replica"),
        P("expert", None),
        P("expert", None),
        P(),
        P("expert", "replica", None, None),
        P("expert", None, "replica"),
    )
    out_specs = P("expert", "replica")
    return jax.shard_map(
        on_device, mesh=mesh, in_specs=in_specs, out_specs=out_specs, check_vma=False
    )
```
